32 devices in a mesh: grp: 4 (over y, x), freq: 8 (over z, core).
Axes of the slice: x: 2, y: 2, z: 4, core: 2. Of those that a mesh axis runs over, the one named last changes fastest.
Arguments:
- transfer: bfloat16 [512, 2, 128, 512], P('freq', None, 'grp'), may hold values from -0.1875 to 0.1875
- adjoint: bfloat16 [512, 2, 512, 128], P('freq'), may hold values from -6 to 6
- lower_rows: bfloat16 [131072, 384], P(('grp', 'freq')), may hold values from -6 to 6
- pivot_store: bfloat16 [512, 384], P('grp'), may hold values from -0.3125 to 0.3125
- owners: int32 [3], replicated, may hold values from 0 to 3
- inverse_factor: bfloat16 [128, 128], replicated, as said below
Outputs:
- panel: bfloat16 [131072, 128], P(('grp', 'freq'))
The draws below stay inside these ranges and needn't reach their ends.
Inputs may be any that keep to these rules, and one draw needn't show every extreme that they name: `inverse_factor`: upper triangular, with diagonal entries from 0.5 to 2.
All inputs are finite; a program needn't handle non-finite values.
Results may differ from the reference program's by a relative error of at most 0.0059.
Values may be sent and summed in bfloat16 or wider, within the bound.
A program may use at most 64 MiB of HBM per device.

```python
import math
import jax
import jax.numpy as jnp
from jax import lax

C = 128
M = 512
NF = 512
PANELS = 3
NT = 1024
NS = 128
N_GRP = 4


def draw_inverse_factor(key, part):
    key = jax.random.fold_in(key, 7)
    diag_key, upper_key = jax.random.split(key)
    diagonal = jnp.exp(jax.random.uniform(diag_key, (C,), jnp.float32, math.log(0.5), math.log(2.0)))
    upper_part = 0.5 * jax.random.normal(upper_key, (C, C), jnp.float32) / math.sqrt(C)
    return (jnp.triu(upper_part, 1) + jnp.diag(diagonal)).astype(jnp.bfloat16)


def block_levels(own_key, dims, pieces, least, high):
    loudness = 1.0
    for dim, shards_of in pieces:
        heights = jax.random.uniform(jax.random.fold_in(jax.random.fold_in(own_key, 6), dim), (shards_of,), jnp.float32, least / len(pieces), high / len(pieces))
        loudness = loudness * jnp.repeat(jnp.exp(heights), dims[dim] // shards_of).reshape((-1,) + (1,) * (len(dims) - 1 - dim))
    return loudness


def centred(own_key, shape, width, bound, cuts=(), kind=jnp.bfloat16):
    gain = block_levels(own_key, shape, cuts, -0.22, 0.18) if cuts else 1.0
    entries = jax.random.normal(own_key, shape, jnp.float32) * width * gain
    return jnp.minimum(jnp.maximum(entries, -bound), bound).astype(kind)


def setup_inputs(seed: int = 0) -> dict:
    key_list = jax.random.split(jax.random.key(seed), 7)
    transfer = centred(key_list[0], (NF, 2, NS, M), (2 * M) ** -0.5, 0.1875, ((0, 8), (2, 4)))
    adjoint = centred(key_list[1], (NF, 2, M, C), 1.0, 6.0, ((0, 8),))
    lower_rows = centred(key_list[2], (NS * NT, PANELS * C), 1.0, 6.0, ((0, 32),))
    pivot_store = centred(key_list[3], (C * N_GRP, PANELS * C), (PANELS * C) ** -0.5, 0.3125, ((0, 4),))
    owners = jax.random.randint(key_list[4], (PANELS,), 0, N_GRP).astype(jnp.int32)
    inverse_factor = draw_inverse_factor(jax.random.fold_in(key_list[6], 71), 0)
    return dict(transfer=transfer, adjoint=adjoint, lower_rows=lower_rows, pivot_store=pivot_store, owners=owners, inverse_factor=inverse_factor)


def make_table(samples, frequencies):
    time_steps = jnp.arange(samples, dtype=jnp.int32)[:, None]
    wave_numbers = jnp.arange(frequencies, dtype=jnp.int32)[None, :]
    phases = (time_steps * wave_numbers % samples).astype(jnp.float32) * (2.0 * math.pi / samples)
    factor = 1.0 / math.sqrt(frequencies)
    return jnp.stack([jnp.cos(phases) * factor, -jnp.sin(phases) * factor]).astype(jnp.bfloat16)

def spectrum(operands):
    trans_pair, adjoint_pair = operands
    trans_pair = trans_pair.astype(jnp.float32)
    adjoint_pair = adjoint_pair.astype(jnp.float32)
    highest = lax.Precision.HIGHEST
    real_part = jnp.dot(trans_pair[0], adjoint_pair[0], precision=highest) - jnp.dot(trans_pair[1], adjoint_pair[1], precision=highest)
    imag_part = jnp.dot(trans_pair[0], adjoint_pair[1], precision=highest) + jnp.dot(trans_pair[1], adjoint_pair[0], precision=highest)
    return jnp.stack([real_part, imag_part], axis=1).astype(jnp.bfloat16)

def reference(transfer, adjoint, lower_rows, pivot_store, owners, inverse_factor):
    spectra = lax.map(spectrum, (transfer, adjoint))
    table = make_table(NT, NF)
    hessian = jnp.einsum('qtk,ksqc->stc', table.astype(jnp.float32), spectra.astype(jnp.float32), precision=lax.Precision.HIGHEST)
    hessian = hessian.reshape(NS * NT, C)
    blocks = []
    for panel_index in range(PANELS):
        row_start = (owners[panel_index] * C).astype(jnp.int32)
        col_start = jnp.asarray(panel_index * C).astype(jnp.int32)
        blocks.append(lax.dynamic_slice(pivot_store, (row_start, col_start), (C, C)))
    pivots = jnp.concatenate(blocks, axis=1)
    update = lax.dot_general(lower_rows, pivots, (((1,), (1,)), ((), ())), preferred_element_type=jnp.float32)
    reduced = (hessian - update).astype(jnp.bfloat16)
    return jnp.dot(reduced, inverse_factor, preferred_element_type=jnp.float32).astype(jnp.bfloat16)
```

```python
import functools
import math

import jax
import jax.numpy as jnp
from jax import lax
from jax.experimental import pallas as pl
from jax.experimental.pallas import tpu as pltpu
from jax.sharding import PartitionSpec as P

MESH = pl.DeviceIdType.MESH
CHUNK = 8
AHEAD = 3
TILE = 256
VMEM_BYTES = 64 * 1024 * 1024
SPARE = 11 * 1024 * 1024
COARSE = 32
QUARTERS = 4


def flip(index, bit):
    return index + bit * (1 - 2 * lax.rem(index // bit, 2))


def kernel(
    nf, ng, kc,
    owners_hbm, tr_hbm, ad_hbm, lo_hbm, pv_hbm, inv_hbm, out_ref,
    owners, tr, ad, lo, pv, inv, spec, sbuf, rbuf, table, acc,
    in_sem, owners_sem, lo_sem, pv_sem, inv_sem, own_sem,
    first_send, first_recv, send_sem, recv_sem, psend_sem, precv_sem,
):
    f32, bf16 = jnp.float32, jnp.bfloat16
    kl, _, sl, _ = tr.shape
    c = ad.shape[3]
    nch = kl // kc
    s_loc = sl // nf
    nt, width = acc.shape
    size = nf // QUARTERS
    me = lax.axis_index("freq")
    grp = lax.axis_index("grp")
    quarter = me // size
    place = lax.rem(me, size)
    end = 1 - lax.rem(quarter // 2 + lax.rem(quarter, 2), 2)
    near = flip(quarter, 1)
    across = flip(quarter, 2)
    other = flip(across, 1)
    far_end = across + end * (other - across)
    far_mid = other + end * (across - other)

    def loads(j):
        rows = pl.ds(j * kc, kc)
        return (
            pltpu.make_async_copy(tr_hbm.at[rows], tr.at[rows], in_sem.at[j, 0]),
            pltpu.make_async_copy(ad_hbm.at[rows], ad.at[rows], in_sem.at[j, 1]),
        )

    lo_copy = pltpu.make_async_copy(lo_hbm, lo, lo_sem)
    owners_copy = pltpu.make_async_copy(owners_hbm, owners, owners_sem)
    pv_copy = pltpu.make_async_copy(pv_hbm, pv.at[grp], pv_sem)
    inv_copy = pltpu.make_async_copy(inv_hbm, inv, inv_sem)

    inv_copy.start()
    for copy in loads(0):
        copy.start()

    barrier = pltpu.get_barrier_semaphore()
    for step in range(1, nf):
        pl.semaphore_signal(
            barrier, inc=1, device_id={"freq": lax.rem(me + step, nf)}, device_id_type=MESH
        )
    for step in range(1, ng):
        pl.semaphore_signal(
            barrier, inc=1, device_id={"grp": lax.rem(grp + step, ng)}, device_id_type=MESH
        )

    def spectra(j):
        for i in range(kc):
            k = j * kc + i
            right = jnp.concatenate([ad[k, 0], ad[k, 1]], axis=1)
            left = jnp.concatenate([tr[k, 0], tr[k, 1]], axis=0)
            both = jnp.dot(left, right, preferred_element_type=f32)
            spec[0, pl.ds(i * sl, sl), :] = both[:sl, :c] - both[sl:, c:]
            spec[1, pl.ds(i * sl, sl), :] = both[:sl, c:] + both[sl:, :c]
        rows = pl.ds(pl.multiple_of(j * 2 * kc, 2 * kc), 2 * kc)
        factor = inv[...]
        for d in range(nf):
            blocks = []
            for s in range(s_loc):
                picked = pl.ds(d * s_loc + s, kc, stride=sl)
                blocks += [spec[0, picked, :], spec[1, picked, :]]
            block = jnp.concatenate(blocks, axis=0).astype(bf16)
            scaled = jnp.dot(block, factor, preferred_element_type=f32).astype(bf16)
            for s in range(s_loc):
                sbuf[d, rows, s * c:(s + 1) * c] = scaled[s * 2 * kc:(s + 1) * 2 * kc, :]

    def device(q, i):
        return q * size + lax.rem(place + i, size)

    def first(j, i):
        dest = device(far_end, i)
        rows = pl.ds(pl.multiple_of(j * 2 * kc, 2 * kc), 2 * kc)
        return pltpu.make_async_remote_copy(
            src_ref=sbuf.at[dest, rows],
            dst_ref=rbuf.at[me, rows],
            send_sem=first_send.at[j, i],
            recv_sem=first_recv.at[end, j, place],
            device_id={"freq": dest},
            device_id_type=MESH,
        )

    def first_arrival(q, kind, j, i):
        src = q * size + i
        rows = pl.ds(pl.multiple_of(j * 2 * kc, 2 * kc), 2 * kc)
        return pltpu.make_async_remote_copy(
            src_ref=sbuf.at[src, rows],
            dst_ref=rbuf.at[src, rows],
            send_sem=first_send.at[j, i],
            recv_sem=first_recv.at[kind, j, i],
            device_id={"freq": src},
            device_id_type=MESH,
        )

    def whole(q, i):
        dest = device(q, i)
        return pltpu.make_async_remote_copy(
            src_ref=sbuf.at[dest],
            dst_ref=rbuf.at[me],
            send_sem=send_sem.at[dest],
            recv_sem=recv_sem.at[me],
            device_id={"freq": dest},
            device_id_type=MESH,
        )

    def whole_arrival(src):
        return pltpu.make_async_remote_copy(
            src_ref=sbuf.at[src],
            dst_ref=rbuf.at[src],
            send_sem=send_sem.at[src],
            recv_sem=recv_sem.at[src],
            device_id={"freq": src},
            device_id_type=MESH,
        )

    own_copy = pltpu.make_async_copy(sbuf.at[me], rbuf.at[me], own_sem)

    def pivot_copy(step, slot):
        return pltpu.make_async_remote_copy(
            src_ref=pv_hbm,
            dst_ref=pv.at[slot],
            send_sem=psend_sem.at[step],
            recv_sem=precv_sem.at[step],
            device_id={"grp": lax.rem(grp + step, ng)},
            device_id_type=MESH,
        )

    inv_copy.wait()
    for copy in loads(0):
        copy.wait()
    for j in range(1, min(AHEAD, nch)):
        for copy in loads(j):
            copy.start()
    spectra(0)
    pl.semaphore_wait(barrier, nf - 1 + ng - 1)
    for i in range(size):
        first(0, i).start()

    @pl.loop(1, nch)
    def _(j):
        @pl.when(j + AHEAD - 1 < nch)
        def _():
            for copy in loads(j + AHEAD - 1):
                copy.start()

        for copy in loads(j):
            copy.wait()
        spectra(j)
        for i in range(size):
            first(j, i).start()

    for i in range(size):
        whole(far_mid, i).start()
    for i in range(size):
        whole(near, i).start()
    for i in range(1, size):
        whole(quarter, i).start()
    own_copy.start()

    owners_copy.start()
    pv_copy.start()
    lo_copy.start()
    for step in range(1, ng):
        pivot_copy(step, grp).start()

    cols = size * 2 * kl
    coarse = nt // COARSE
    scale = 1.0 / math.sqrt(kl * nf)
    turn = 2.0 * math.pi / nt

    @pl.loop(0, QUARTERS)
    def _(q):
        def phase(rows, step, shift):
            col = lax.broadcasted_iota(jnp.int32, (rows, cols), 1)
            row = lax.broadcasted_iota(jnp.int32, (rows, cols), 0) * step
            kk = q * size * kl + (col // (2 * kc)) * kc + col % kc
            part = (col // kc) % 2
            turns = kk * row + part * shift
            return (turns % nt).astype(f32) * turn

        high = phase(coarse, COARSE, 0)
        low = phase(COARSE, 1, nt // 4)
        cos_high, sin_high = jnp.cos(high) * scale, jnp.sin(high) * scale
        cos_low, sin_low = jnp.cos(low), jnp.sin(low)
        for a in range(coarse):
            value = cos_high[a:a + 1] * cos_low - sin_high[a:a + 1] * sin_low
            table[q, a * COARSE:(a + 1) * COARSE, :] = value.astype(bf16)

    lo_copy.wait()
    owners_copy.wait()
    pv_copy.wait()
    for step in range(1, ng):
        pivot_copy(step, lax.rem(grp + ng - step, ng)).wait_recv()
    panels = lo.shape[1] // c
    pivots = jnp.concatenate(
        [pv[owners[p], :, p * c:(p + 1) * c] for p in range(panels)], axis=1
    )
    turned = jnp.transpose(inv[...].astype(f32)).astype(bf16)
    scaled_pivots = jnp.dot(turned, pivots, preferred_element_type=f32).astype(bf16)
    tile = min(TILE, nt)

    for s in range(s_loc):
        @pl.loop(0, nt // tile)
        def _(i):
            rows = lo[pl.ds(pl.multiple_of(s * nt + i * tile, tile), tile), :]
            update = lax.dot_general(
                rows, scaled_pivots, (((1,), (1,)), ((), ())), preferred_element_type=f32
            )
            acc[pl.ds(pl.multiple_of(i * tile, tile), tile), s * c:(s + 1) * c] = -update

    def term(q, i):
        rows = pl.ds(pl.multiple_of(i * tile, tile), tile)
        right = rbuf[pl.ds(q * size, size)].reshape(cols, width)
        return acc[rows, :] + jnp.dot(table[q, rows, :], right, preferred_element_type=f32)

    def add(q):
        @pl.loop(0, nt // tile)
        def _(i):
            acc[pl.ds(pl.multiple_of(i * tile, tile), tile), :] = term(q, i)

    def wait_whole(q):
        for i in range(size):
            whole_arrival(q * size + i).wait_recv()

    def wait_first(q, kind):
        @pl.loop(0, nch)
        def _(j):
            for i in range(size):
                first_arrival(q, kind, j, i).wait_recv()

    own_copy.wait()
    for i in range(1, size):
        whole_arrival(device(quarter, i)).wait_recv()
    add(quarter)

    wait_whole(near)
    add(near)

    @pl.when(end == 1)
    def _():
        wait_first(far_end, 1)

    @pl.when(end == 0)
    def _():
        wait_whole(far_end)
    add(far_end)

    @pl.when(end == 1)
    def _():
        wait_first(far_mid, 0)

    @pl.when(end == 0)
    def _():
        wait_whole(far_mid)

    @pl.loop(0, nt // tile)
    def _(i):
        value = term(far_mid, i).astype(bf16)
        for s in range(s_loc):
            out_ref[pl.ds(pl.multiple_of(s * nt + i * tile, tile), tile), :] = value[:, s * c:(s + 1) * c]

    @pl.loop(0, nch)
    def _(j):
        for i in range(size):
            first(j, i).wait_send()
    for i in range(size):
        whole(far_mid, i).wait_send()
        whole(near, i).wait_send()
    for i in range(1, size):
        whole(quarter, i).wait_send()
    for step in range(1, ng):
        pivot_copy(step, grp).wait_send()


def per_device(nf, ng, transfer, adjoint, lower_rows, pivot_store, owners, inverse_factor):
    kl, _, sl, m = transfer.shape
    c = adjoint.shape[3]
    kc = min(CHUNK, kl)
    nch = kl // kc
    s_loc = sl // nf
    size = nf // QUARTERS
    rows = lower_rows.shape[0]
    nt = rows // s_loc
    bf16 = jnp.bfloat16
    in_hbm = lambda x: pltpu.with_memory_space_constraint(x, pltpu.HBM)
    dma = pltpu.SemaphoreType.DMA
    return pl.pallas_call(
        functools.partial(kernel, nf, ng, kc),
        out_shape=jax.ShapeDtypeStruct((rows, c), bf16),
        in_specs=[pl.BlockSpec(memory_space=pltpu.HBM)] * 6,
        out_specs=pl.BlockSpec(memory_space=pltpu.VMEM),
        scratch_shapes=[
            pltpu.SMEM(owners.shape, jnp.int32),
            pltpu.VMEM(transfer.shape, bf16),
            pltpu.VMEM(adjoint.shape, bf16),
            pltpu.VMEM(lower_rows.shape, bf16),
            pltpu.VMEM((ng,) + pivot_store.shape, bf16),
            pltpu.VMEM(inverse_factor.shape, bf16),
            pltpu.VMEM((2, kc * sl, c), jnp.float32),
            pltpu.VMEM((nf, 2 * kl, s_loc * c), bf16),
            pltpu.VMEM((nf, 2 * kl, s_loc * c), bf16),
            pltpu.VMEM((QUARTERS, nt, size * 2 * kl), bf16),
            pltpu.VMEM((nt, s_loc * c), jnp.float32),
            dma((nch, 2)), dma, dma, dma, dma, dma,
            dma((nch, size)), dma((2, nch, size)), dma((nf,)), dma((nf,)), dma((ng,)), dma((ng,)),
        ],
        compiler_params=pltpu.CompilerParams(
            collective_id=0, has_side_effects=True, vmem_limit_bytes=VMEM_BYTES - 2 * rows * c - SPARE
        ),
    )(in_hbm(owners), transfer, adjoint, lower_rows, in_hbm(pivot_store), in_hbm(inverse_factor))


def solution(mesh):
    nf, ng = mesh.shape["freq"], mesh.shape["grp"]
    in_specs = (
        P("freq", None, "grp", None),
        P("freq", None, None, None),
        P(("grp", "freq"), None),
        P("grp", None),
        P(),
        P(),
    )
    out_specs = P(("grp", "freq"), None)
    return jax.shard_map(
        functools.partial(per_device, nf, ng),
        mesh=mesh, in_specs=in_specs, out_specs=out_specs, check_vma=False,
    )
```

```python
import functools
import math

import jax
import jax.numpy as jnp
from jax import lax
from jax.experimental import pallas as pl
from jax.experimental.pallas import tpu as pltpu
from jax.sharding import PartitionSpec as P

MESH = pl.DeviceIdType.MESH
CHUNK = 8
AHEAD = 4
PARTS = 4
HALVES = 2
LEAD = 2
NEAR_MESSAGES = 4
TILE = 1024
VMEM_BYTES = 64 * 1024 * 1024
SPARE = 11 * 1024 * 1024
LAST_BYTES = 4 * 1024 * 1024
COARSE = 32
QUARTERS = 4


def flip(index, bit):
    return index + bit * (1 - 2 * lax.rem(index // bit, 2))


def half_block(ref, q, h, size):
    block = ref[pl.ds(q * size, size), h]
    return block.reshape(block.shape[0] * block.shape[1], block.shape[2])


def finished(acc, table, rbuf, q, h, size):
    part = acc.shape[1] // HALVES
    right = half_block(rbuf, q, h, size)
    return acc[:, h * part:(h + 1) * part] + jnp.dot(table[...], right, preferred_element_type=jnp.float32)


def last_kernel(nf, done, acc, table, rbuf, out_hbm, staged, sem):
    size = nf // QUARTERS
    quarter = lax.axis_index("freq") // size
    far_mid = 1 + 1 - quarter // 2
    nt = acc.shape[0]
    c = out_hbm.shape[1]
    rows = done.shape[0]

    first = pltpu.make_async_copy(done, out_hbm.at[pl.ds(0, rows)], sem.at[0])
    first.start()
    copies = [first]
    part = acc.shape[1] // HALVES
    for h in range(1, HALVES):
        right = half_block(rbuf, far_mid, h, size)
        for s in range(part // c):
            low = h * part + s * c
            block = acc[:, low:low + c] + jnp.dot(
                table[...], right[:, s * c:(s + 1) * c], preferred_element_type=jnp.float32
            )
            place = low // c * nt
            staged[place - rows:place - rows + nt, :] = block.astype(staged.dtype)
            copy = pltpu.make_async_copy(
                staged.at[pl.ds(place - rows, nt)], out_hbm.at[pl.ds(place, nt)], sem.at[len(copies)]
            )
            copy.start()
            copies.append(copy)
    for copy in copies:
        copy.wait()


def kernel(
    nf, ng, kc,
    owners_hbm, tr_hbm, ad_hbm, lo_hbm, pv_hbm, inv_hbm, done, acc, last_table, rbuf,
    owners, tr, ad, lo, pv, inv, spec, sbuf, table,
    joined, known, ready, part_sem, in_sem, owners_sem, lo_sem, pv_sem, inv_sem, own_sem,
    send_sem, recv_sem, psend_sem, precv_sem,
):
    f32, bf16 = jnp.float32, jnp.bfloat16
    kl, _, sl, _ = tr.shape
    c = ad.shape[3]
    nch = kl // kc
    s_loc = sl // nf
    nt, width = acc.shape
    size = nf // QUARTERS
    me = lax.axis_index("freq")
    grp = lax.axis_index("grp")
    quarter = me // size
    place = lax.rem(me, size)
    end = 1 - lax.rem(quarter // 2 + lax.rem(quarter, 2), 2)
    near = flip(quarter, 1)
    across = flip(quarter, 2)
    other = flip(across, 1)
    far_end = across + end * (other - across)
    far_mid = other + end * (across - other)
    early = 2 * (1 - quarter // 2)
    late = early + 1
    odd = lax.rem(quarter, 2)

    def device(q, i):
        return q * size + lax.rem(place + i, size)

    part = max(1, kc // PARTS)

    def first_loads(p):
        rows = pl.ds(p * part, part)
        return (
            pltpu.make_async_copy(tr_hbm.at[rows], tr.at[rows], part_sem.at[p, 0]),
            pltpu.make_async_copy(ad_hbm.at[rows], ad.at[rows], part_sem.at[p, 1]),
        )

    def loads(j):
        rows = pl.ds(j * kc, kc)
        return (
            pltpu.make_async_copy(tr_hbm.at[rows], tr.at[rows], in_sem.at[j, 0]),
            pltpu.make_async_copy(ad_hbm.at[rows], ad.at[rows], in_sem.at[j, 1]),
        )

    lo_copy = pltpu.make_async_copy(lo_hbm, lo, lo_sem)
    owners_copy = pltpu.make_async_copy(owners_hbm, owners, owners_sem)
    pv_copy = pltpu.make_async_copy(pv_hbm, pv.at[grp], pv_sem)
    inv_copy = pltpu.make_async_copy(inv_hbm, inv, inv_sem)

    for p in range(kc // part):
        for copy in first_loads(p):
            copy.start()
    inv_copy.start()

    barrier = pltpu.get_barrier_semaphore()

    def greet(sem, q, skip=0):
        for i in range(skip, size):
            pl.semaphore_signal(sem, inc=1, device_id={"freq": device(q, i)}, device_id_type=MESH)

    def greet_groups(sem):
        for step in range(1, ng):
            pl.semaphore_signal(
                sem, inc=1, device_id={"grp": lax.rem(grp + step, ng)}, device_id_type=MESH
            )

    greet(barrier, across)
    greet(barrier, other)
    greet(barrier, quarter, 1)

    @pl.when(end == 0)
    def _():
        greet(barrier, near)

    @pl.when(end == 1)
    def _():
        greet_groups(barrier)

    def spectra(j, parts=False):
        for i in range(kc):
            if parts and i % part == 0:
                for copy in first_loads(i // part):
                    copy.wait()
            k = j * kc + i
            right = jnp.concatenate([ad[k, 0], ad[k, 1]], axis=1)
            left = jnp.concatenate([tr[k, 0], tr[k, 1]], axis=0)
            both = jnp.dot(left, right, preferred_element_type=f32)
            spec[0, pl.ds(i * sl, sl), :] = both[:sl, :c] - both[sl:, c:]
            spec[1, pl.ds(i * sl, sl), :] = both[:sl, c:] + both[sl:, :c]
        if parts:
            inv_copy.wait()

    def pack(j, d):
        rows = pl.ds(pl.multiple_of(j * 2 * kc, 2 * kc), 2 * kc)
        blocks = []
        for s in range(s_loc):
            picked = pl.ds(d * s_loc + s, kc, stride=sl)
            blocks += [spec[0, picked, :], spec[1, picked, :]]
        block = jnp.concatenate(blocks, axis=0).astype(bf16)
        scaled = jnp.dot(block, inv[...], preferred_element_type=f32).astype(bf16)
        for s in range(s_loc):
            h, column = s // (s_loc // HALVES), s % (s_loc // HALVES) * c
            sbuf[d, h, rows, column:column + c] = scaled[s * 2 * kc:(s + 1) * 2 * kc, :]

    def pack_first(j):
        for i in range(size):
            pack(j, device(early, i))

    def pack_rest(j):
        for q in (late, near, quarter):
            for i in range(size):
                pack(j, device(q, i))

    def send(q, i, which, index):
        dest = device(q, i)
        return pltpu.make_async_remote_copy(
            src_ref=sbuf.at[(dest, *index)],
            dst_ref=rbuf.at[(me, *index)],
            send_sem=send_sem.at[dest, which],
            recv_sem=recv_sem.at[me, which],
            device_id={"freq": dest},
            device_id_type=MESH,
        )

    def arrival(src, which, index):
        return pltpu.make_async_remote_copy(
            src_ref=sbuf.at[(src, *index)],
            dst_ref=rbuf.at[(src, *index)],
            send_sem=send_sem.at[src, which],
            recv_sem=recv_sem.at[src, which],
            device_id={"freq": src},
            device_id_type=MESH,
        )

    everything = slice(None)

    def chunk_rows(j, n=1):
        return (everything, pl.ds(pl.multiple_of(j * 2 * kc, 2 * kc), n * 2 * kc))

    lead = min(LEAD, nch - 1)
    head = (everything, pl.ds(0, lead * 2 * kc))

    def tail(h, n):
        return (h, pl.ds(n * 2 * kc, (nch - n) * 2 * kc))

    def send_group(q, j, which, n=1):
        for i in range(size):
            send(q, i, which, chunk_rows(j, n)).start()

    def send_tails(n):
        for h in range(HALVES):
            for i in range(size):
                send(late, i, h, tail(h, n)).start()

    def late_index(n):
        return [(h, tail(h, n)) for h in range(HALVES)] + ([(HALVES, head)] if n else [])

    own_copy = pltpu.make_async_copy(sbuf.at[me], rbuf.at[me], own_sem)

    def pivot_copy(step, slot):
        return pltpu.make_async_remote_copy(
            src_ref=pv_hbm,
            dst_ref=pv.at[slot],
            send_sem=psend_sem.at[step],
            recv_sem=precv_sem.at[step],
            device_id={"grp": lax.rem(grp + step, ng)},
            device_id_type=MESH,
        )

    for j in range(1, min(AHEAD, nch)):
        for copy in loads(j):
            copy.start()
    group = max(1, nch // NEAR_MESSAGES)

    def sends(j):
        send_group(early, j, 0)
        if lead:
            @pl.when(end == 0)
            def _():
                @pl.when(j < lead)
                def _():
                    send_group(late, j, HALVES)

        @pl.when(lax.rem(j, group) == group - 1)
        def _():
            @pl.when(jnp.logical_and(end == 0, j == group - 1))
            def _():
                pl.semaphore_wait(ready, size)
            send_group(near, j - (group - 1), 0, group)

    spectra(0, parts=True)
    pack_first(0)
    pack_rest(0)
    pl.semaphore_wait(barrier, nf - 1 + end * (ng - 1) - (1 - end) * size)

    @pl.when(end == 1)
    def _():
        greet(ready, near)
        greet_groups(joined)

    @pl.loop(0, nch)
    def _(j):
        @pl.when(j > 0)
        def _():
            @pl.when(j + AHEAD - 1 < nch)
            def _():
                for copy in loads(j + AHEAD - 1):
                    copy.start()

            for copy in loads(j):
                copy.wait()
            spectra(j)
            pack_first(j)
            pack_rest(j)
        sends(j)

    @pl.when(end == 1)
    def _():
        send_tails(0)

    @pl.when(end == 0)
    def _():
        send_tails(lead)

    @pl.when(end == 1)
    def _():
        pl.semaphore_wait(joined, ng - 1)
        greet(known, near)

    @pl.when(end == 0)
    def _():
        pl.semaphore_wait(known, size)

    for i in range(1, size):
        send(quarter, i, 0, (everything,)).start()
    own_copy.start()

    owners_copy.start()
    pv_copy.start()
    lo_copy.start()
    for step in range(1, ng):
        pivot_copy(step, grp).start()

    cols = size * 2 * kl
    coarse = nt // COARSE
    scale = 1.0 / math.sqrt(kl * nf)
    turn = 2.0 * math.pi / nt

    def make_table(q, ref):
        def phase(rows, step, shift):
            col = lax.broadcasted_iota(jnp.int32, (rows, cols), 1)
            row = lax.broadcasted_iota(jnp.int32, (rows, cols), 0) * step
            kk = q * size * kl + (col // (2 * kc)) * kc + col % kc
            imaginary = (col // kc) % 2
            turns = kk * row + imaginary * shift
            return (turns % nt).astype(f32) * turn

        high = phase(coarse, COARSE, 0)
        low = phase(COARSE, 1, nt // 4)
        cos_high, sin_high = jnp.cos(high) * scale, jnp.sin(high) * scale
        cos_low, sin_low = jnp.cos(low), jnp.sin(low)
        for a in range(coarse):
            value = cos_high[a:a + 1] * cos_low - sin_high[a:a + 1] * sin_low
            ref[a * COARSE:(a + 1) * COARSE, :] = value.astype(bf16)

    @pl.loop(0, QUARTERS)
    def _(q):
        make_table(q, table.at[q])
    make_table(far_mid, last_table)

    lo_copy.wait()
    owners_copy.wait()
    pv_copy.wait()
    for step in range(1, ng):
        pivot_copy(step, lax.rem(grp + ng - step, ng)).wait_recv()
    panels = lo.shape[1] // c
    pivots = jnp.concatenate(
        [pv[owners[p], :, p * c:(p + 1) * c] for p in range(panels)], axis=1
    )
    turned = jnp.transpose(inv[...].astype(f32)).astype(bf16)
    scaled_pivots = jnp.dot(turned, pivots, preferred_element_type=f32).astype(bf16)
    tile = min(TILE, nt)

    for s in range(s_loc):
        @pl.loop(0, nt // tile)
        def _(i):
            rows = lo[pl.ds(pl.multiple_of(s * nt + i * tile, tile), tile), :]
            update = lax.dot_general(
                rows, scaled_pivots, (((1,), (1,)), ((), ())), preferred_element_type=f32
            )
            acc[pl.ds(pl.multiple_of(i * tile, tile), tile), s * c:(s + 1) * c] = -update

    def term(q, i):
        rows = pl.ds(pl.multiple_of(i * tile, tile), tile)
        right = jnp.concatenate([half_block(rbuf, q, h, size) for h in range(HALVES)], axis=1)
        return acc[rows, :] + jnp.dot(table[q, rows, :], right, preferred_element_type=f32)

    def add(q):
        @pl.loop(0, nt // tile)
        def _(i):
            acc[pl.ds(pl.multiple_of(i * tile, tile), tile), :] = term(q, i)

    def wait_all(q):
        for i in range(size):
            arrival(q * size + i, 0, (everything,)).wait_recv()

    def wait_half(q, h, n):
        for i in range(size):
            if n and h == 0:
                arrival(q * size + i, HALVES, head).wait_recv()
            arrival(q * size + i, h, tail(h, n)).wait_recv()

    own_copy.wait()
    for i in range(1, size):
        arrival(device(quarter, i), 0, (everything,)).wait_recv()
    add(quarter)

    wait_all(near)
    add(near)

    @pl.when(odd == 0)
    def _():
        wait_all(far_end)

    @pl.when(odd == 1)
    def _():
        for h in range(HALVES):
            wait_half(far_end, h, 0)
    add(far_end)

    for i in range(size):
        for q in (early, near):
            send(q, i, 0, (everything,)).wait_send()
    for i in range(1, size):
        send(quarter, i, 0, (everything,)).wait_send()

    @pl.when(odd == 0)
    def _():
        wait_all(far_mid)

    @pl.when(odd == 1)
    def _():
        wait_half(far_mid, 0, lead)

    part_width = width // HALVES
    value = finished(acc, last_table, rbuf, far_mid, 0, size).astype(bf16)
    for s in range(part_width // c):
        done[s * nt:(s + 1) * nt, :] = value[:, s * c:(s + 1) * c]

    @pl.when(odd == 1)
    def _():
        for h in range(1, HALVES):
            wait_half(far_mid, h, lead)

    @pl.when(end == 1)
    def _():
        for i in range(size):
            for which, index in late_index(0):
                send(late, i, which, index).wait_send()

    @pl.when(end == 0)
    def _():
        for i in range(size):
            for which, index in late_index(lead):
                send(late, i, which, index).wait_send()
    for step in range(1, ng):
        pivot_copy(step, grp).wait_send()


def per_device(nf, ng, transfer, adjoint, lower_rows, pivot_store, owners, inverse_factor):
    kl, _, sl, m = transfer.shape
    c = adjoint.shape[3]
    kc = min(CHUNK, kl)
    nch = kl // kc
    s_loc = sl // nf
    size = nf // QUARTERS
    rows = lower_rows.shape[0]
    nt = rows // s_loc
    bf16 = jnp.bfloat16
    in_hbm = lambda x: pltpu.with_memory_space_constraint(x, pltpu.HBM)
    dma = pltpu.SemaphoreType.DMA
    width = s_loc * c
    cols = size * 2 * kl
    vmem = pl.BlockSpec(memory_space=pltpu.VMEM)
    outs = [
        jax.ShapeDtypeStruct((rows // HALVES, c), bf16),
        jax.ShapeDtypeStruct((nt, width), jnp.float32),
        jax.ShapeDtypeStruct((nt, cols), bf16),
        jax.ShapeDtypeStruct((nf, HALVES, 2 * kl, width // HALVES), bf16),
    ]
    held = sum(math.prod(out.shape) * out.dtype.itemsize for out in outs)
    parts = pl.pallas_call(
        functools.partial(kernel, nf, ng, kc),
        out_shape=outs,
        in_specs=[pl.BlockSpec(memory_space=pltpu.HBM)] * 6,
        out_specs=[vmem] * len(outs),
        scratch_shapes=[
            pltpu.SMEM(owners.shape, jnp.int32),
            pltpu.VMEM(transfer.shape, bf16),
            pltpu.VMEM(adjoint.shape, bf16),
            pltpu.VMEM(lower_rows.shape, bf16),
            pltpu.VMEM((ng,) + pivot_store.shape, bf16),
            pltpu.VMEM(inverse_factor.shape, bf16),
            pltpu.VMEM((2, kc * sl, c), jnp.float32),
            pltpu.VMEM((nf, HALVES, 2 * kl, width // HALVES), bf16),
            pltpu.VMEM((QUARTERS, nt, cols), bf16),
            pltpu.SemaphoreType.REGULAR,
            pltpu.SemaphoreType.REGULAR,
            pltpu.SemaphoreType.REGULAR,
            dma((PARTS, 2)), dma((nch, 2)), dma, dma, dma, dma, dma,
            dma((nf, HALVES + 1)), dma((nf, HALVES + 1)), dma((ng,)), dma((ng,)),
        ],
        compiler_params=pltpu.CompilerParams(
            collective_id=0, has_side_effects=True, vmem_limit_bytes=VMEM_BYTES - held - SPARE
        ),
    )(in_hbm(owners), transfer, adjoint, lower_rows, in_hbm(pivot_store), in_hbm(inverse_factor))
    return pl.pallas_call(
        functools.partial(last_kernel, nf),
        out_shape=jax.ShapeDtypeStruct((rows, c), bf16),
        in_specs=[vmem] * len(outs),
        out_specs=pl.BlockSpec(memory_space=pltpu.HBM),
        scratch_shapes=[pltpu.VMEM((rows - rows // HALVES, c), bf16), dma((1 + s_loc,))],
        compiler_params=pltpu.CompilerParams(vmem_limit_bytes=LAST_BYTES),
    )(*parts)


def solution(mesh):
    nf, ng = mesh.shape["freq"], mesh.shape["grp"]
    in_specs = (
        P("freq", None, "grp", None),
        P("freq", None, None, None),
        P(("grp", "freq"), None),
        P("grp", None),
        P(),
        P(),
    )
    out_specs = P(("grp", "freq"), None)
    return jax.shard_map(
        functools.partial(per_device, nf, ng),
        mesh=mesh, in_specs=in_specs, out_specs=out_specs, check_vma=False,
    )
```
